512 devices in a mesh: batch: 32 (over z, core), row: 4 (over y), col: 4 (over x).
Axes of the slice: x: 4, y: 4, z: 16, core: 2. Of those that a mesh axis runs over, the one named last changes fastest.
Arguments:
- image_tokens: bfloat16 [128, 256, 3072], P('batch', ('row', 'col')), may hold values from -36 to 36
- text_tokens: bfloat16 [128, 128, 3072], P('batch', ('row', 'col')), may hold values from -36 to 36
- modulation: float32 [128, 7, 3072], P('batch'), may hold values from -3.5 to 3.5
- qkv_weight: bfloat16 [3072, 12, 384], P('col', 'row'), may hold values from -0.109375 to 0.109375
- kv_weight: bfloat16 [3072, 12, 256], P('col', 'row'), may hold values from -0.109375 to 0.109375
- norm_gains: float32 [3, 128], replicated, may hold values from 1 to 2.2
- out_weight: bfloat16 [12, 128, 3072], P('row', None, 'col'), may hold values from -0.15625 to 0.15625
- final_weight: bfloat16 [3072, 64], replicated, may hold values from -0.109375 to 0.109375
- text_lengths: int32 [128], P('batch'), may hold values from 1 to 128, as said below
- partner: int32 [128], P('batch'), may hold values from 0 to 127, as said below
- guidance: float32 [128], P('batch'), may hold values from 1.5 to 4.5
- step_size: float32 [128], P('batch'), may hold values from -0.3 to -0.05
- latent: float32 [128, 256, 64], P('batch', ('row', 'col')), may hold values from -6 to 6
Outputs:
- next_latent: float32 [128, 256, 64], P('batch', ('row', 'col'))
The draws below stay inside these ranges and needn't reach their ends.
Inputs may be any that keep to these rules, and one draw needn't show every extreme that they name: `text_lengths`: some sequence has all 128 text tokens live. partner[partner[s]] = s and partner[s] != s for every sequence s.
All inputs are finite; a program needn't handle non-finite values.
Results may differ from the reference program's by a relative error of at most 0.007.
Values may be sent and summed in bfloat16 or wider, within the bound.
No kernel may reach another device: no remote copies, remote signals or barrier semaphores. Data moves between devices by JAX's collectives and lax.ppermute only.
A program may use at most 64 MiB of HBM per device.

```python
import math
import jax
import jax.numpy as jnp
from jax import lax

D = 3072
HD = 128
C = 64
H = 12
IMG_TOK = 256
TXT_LEN = 128
SEQS = 128
N_ROW = 4
N_COL = 4


def scaled_states(key, rows):
    first, second, third = jax.random.split(key, 3)
    feature_scale = jnp.exp(jax.random.uniform(first, (D,), jnp.float32, jnp.log(0.3), jnp.log(3.0)))
    row_scale = jnp.exp(jax.random.uniform(second, (SEQS, rows, 1), jnp.float32, jnp.log(0.3), jnp.log(3.0)))
    base = jnp.clip(jax.random.normal(third, (SEQS, rows, D), jnp.float32), -4.0, 4.0)
    return (base * feature_scale * row_scale).astype(jnp.bfloat16)


def draw_image_tokens(key, part):
    return scaled_states(jax.random.fold_in(key, 11), IMG_TOK)


def draw_text_tokens(key, part):
    return scaled_states(jax.random.fold_in(key, 23), TXT_LEN)


def draw_text_lengths(key, part):
    first, second = jax.random.split(jax.random.fold_in(key, 37))
    lengths = jax.random.randint(first, (SEQS,), 1, TXT_LEN + 1, jnp.int32)
    chosen = jax.random.randint(second, (), 0, SEQS, jnp.int32)
    return lengths.at[chosen].set(TXT_LEN)


def draw_partner(key, part):
    order = jax.random.permutation(jax.random.fold_in(key, 41), jnp.arange(SEQS, dtype=jnp.int32))
    firsts = order[0::2]
    seconds = order[1::2]
    paired = jnp.zeros((SEQS,), jnp.int32)
    paired = paired.at[firsts].set(seconds)
    return paired.at[seconds].set(firsts)


def block_levels(key, shape, pieces, low, top_value):
    def one(dim, parts):
        heights = jax.random.uniform(jax.random.fold_in(jax.random.fold_in(key, 6), dim), (parts,), jnp.float32, low / len(pieces), top_value / len(pieces))
        return jnp.repeat(jnp.exp(heights), shape[dim] // parts).reshape((-1,) + (1,) * (len(shape) - dim - 1))

    factor_of = one(*pieces[0])
    for cut in pieces[1:]:
        factor_of = factor_of * one(*cut)
    return factor_of


def bell_draw(own_key, shape, width, reach, cuts=(), held_as=jnp.bfloat16):
    array = width * jax.random.normal(own_key, shape, jnp.float32)
    if cuts:
        array = array * block_levels(own_key, shape, cuts, -0.22, 0.18)
    return jnp.clip(array, -reach, reach).astype(held_as)


def setup_inputs(seed: int = 0) -> dict:
    keys = jax.random.split(jax.random.key(seed), 14)
    image_tokens = draw_image_tokens(jax.random.fold_in(keys[13], 71), 0)
    text_tokens = draw_text_tokens(jax.random.fold_in(keys[13], 71), 0)
    modulation = bell_draw(keys[2], (SEQS, 7, D), 0.7, 3.5, ((0, 32),), jnp.float32)
    qkv_weight = bell_draw(keys[3], (D, H, 3 * HD), D ** -0.5, 0.109375, ((0, 4), (1, 4)))
    kv_weight = bell_draw(keys[4], (D, H, 2 * HD), D ** -0.5, 0.109375, ((0, 4), (1, 4)))
    norm_gains = jnp.clip(jnp.exp(jax.random.uniform(keys[5], (3, HD), jnp.float32, math.log(1.0), math.log(2.2))), 1.0, 2.2)
    out_weight = bell_draw(keys[6], (H, HD, D), (H * HD) ** -0.5, 0.15625, ((0, 4), (2, 4)))
    final_weight = bell_draw(keys[7], (D, C), D ** -0.5, 0.109375)
    text_lengths = draw_text_lengths(jax.random.fold_in(keys[13], 71), 0)
    partner = draw_partner(jax.random.fold_in(keys[13], 71), 0)
    guidance = jnp.clip(1.5 + 3.0 * jax.random.uniform(keys[10], (SEQS,), jnp.float32) ** block_levels(keys[10], (SEQS,), ((0, 32),), -0.2, 0.2), 1.5, 4.5)
    step_size = jnp.clip(-0.3 + 0.25 * jax.random.uniform(keys[11], (SEQS,), jnp.float32) ** block_levels(keys[11], (SEQS,), ((0, 32),), -0.2, 0.2), -0.3, -0.05)
    latent = bell_draw(keys[12], (SEQS, IMG_TOK, C), 1.0, 6.0, ((0, 32), (1, 16)), jnp.float32)
    return dict(image_tokens=image_tokens, text_tokens=text_tokens, modulation=modulation, qkv_weight=qkv_weight, kv_weight=kv_weight, norm_gains=norm_gains, out_weight=out_weight, final_weight=final_weight, text_lengths=text_lengths, partner=partner, guidance=guidance, step_size=step_size, latent=latent)


epsilon = 1e-06

def layer_norm(values):
    center = lax.optimization_barrier(jnp.mean(values, axis=-1, keepdims=True))
    spread = lax.optimization_barrier(jnp.mean((values - center) * (values - center), axis=-1, keepdims=True))
    return (values - center) * lax.rsqrt(spread + epsilon)

def modulate(values, shift, scale):
    return layer_norm(values) * (1.0 + scale) + shift

def head_norm(values, gain):
    return values * lax.rsqrt(lax.optimization_barrier(jnp.mean(values * values, axis=-1, keepdims=True)) + epsilon) * gain

def rounded_sum(terms):
    narrow = lax.optimization_barrier(terms.astype(jnp.bfloat16))
    return lax.optimization_barrier(jnp.sum(narrow.astype(jnp.float32), axis=0))

def reference(image_tokens, text_tokens, modulation, qkv_weight, kv_weight, norm_gains, out_weight, final_weight, text_lengths, partner, guidance, step_size, latent):
    block_width = D // N_COL
    head_group = H // N_ROW
    qkv_blocks = qkv_weight.reshape(N_COL, block_width, H, 3 * HD).astype(jnp.float32)
    kv_blocks = kv_weight.reshape(N_COL, block_width, H, 2 * HD).astype(jnp.float32)
    out_blocks = out_weight.reshape(N_ROW, head_group * HD, D).astype(jnp.float32)

    def one_sequence(inputs):
        image_seq, text_seq, mods, length = inputs
        image_mod = modulate(image_seq.astype(jnp.float32), mods[0], mods[1]).astype(jnp.bfloat16)
        text_mod = modulate(text_seq.astype(jnp.float32), mods[3], mods[4]).astype(jnp.bfloat16)
        image_split = image_mod.reshape(IMG_TOK, N_COL, block_width).astype(jnp.float32)
        text_split = text_mod.reshape(TXT_LEN, N_COL, block_width).astype(jnp.float32)
        qkv = rounded_sum(jnp.einsum('tcd,cdhe->cthe', image_split, qkv_blocks))
        kv = rounded_sum(jnp.einsum('tcd,cdhe->cthe', text_split, kv_blocks))
        queries = head_norm(qkv[..., :HD], norm_gains[0]).astype(jnp.bfloat16)
        image_keys = head_norm(qkv[..., HD:2 * HD], norm_gains[1]).astype(jnp.bfloat16)
        image_values = qkv[..., 2 * HD:].astype(jnp.bfloat16)
        text_keys = head_norm(kv[..., :HD], norm_gains[2]).astype(jnp.bfloat16)
        text_values = kv[..., HD:].astype(jnp.bfloat16)
        all_keys = jnp.concatenate([text_keys, image_keys], axis=0)
        all_values = jnp.concatenate([text_values, image_values], axis=0)
        live = jnp.concatenate([(jnp.arange(TXT_LEN, dtype=jnp.int32) < length).astype(jnp.float32), jnp.ones((IMG_TOK,), jnp.float32)])
        scores = jnp.einsum('qhe,khe->hqk', queries.astype(jnp.float32), all_keys.astype(jnp.float32)) / math.sqrt(HD)
        expo = jnp.exp(scores) * live[None, None, :]
        totals = lax.optimization_barrier(jnp.sum(expo, axis=-1))
        mixed = jnp.einsum('hqk,khe->qhe', expo.astype(jnp.bfloat16).astype(jnp.float32), all_values.astype(jnp.float32))
        heads = (mixed / jnp.transpose(totals)[:, :, None]).astype(jnp.bfloat16)
        head_split = heads.reshape(IMG_TOK, N_ROW, head_group * HD).astype(jnp.float32)
        attn = rounded_sum(jnp.einsum('tre,red->rtd', head_split, out_blocks)).astype(jnp.bfloat16)
        residual = image_seq.astype(jnp.float32) + mods[2] * attn.astype(jnp.float32)
        final_in = modulate(residual, mods[5], mods[6]).astype(jnp.bfloat16)
        return jnp.dot(final_in, final_weight, preferred_element_type=jnp.float32)
    velocity = lax.map(one_sequence, (image_tokens, text_tokens, modulation, text_lengths))
    is_cond = jnp.arange(SEQS, dtype=jnp.int32) < partner
    mate = jnp.take(velocity, partner, axis=0)
    cond_vel = jnp.where(is_cond[:, None, None], velocity, mate)
    uncond_vel = jnp.where(is_cond[:, None, None], mate, velocity)
    scale_guide = jnp.where(is_cond, guidance, jnp.take(guidance, partner))
    guided = uncond_vel + scale_guide[:, None, None] * (cond_vel - uncond_vel)
    ratio = jnp.sqrt((lax.optimization_barrier(jnp.mean(cond_vel * cond_vel, axis=-1, keepdims=True)) + epsilon) / (lax.optimization_barrier(jnp.mean(guided * guided, axis=-1, keepdims=True)) + epsilon))
    return latent + step_size[:, None, None] * guided * (0.7 * ratio + 0.3)
```

```python
import functools
import math

import jax
import jax.numpy as jnp
from jax import lax
from jax.experimental import pallas as pl
from jax.experimental.pallas import tpu as pltpu
from jax.sharding import PartitionSpec as P


epsilon = 1e-06
F32 = jnp.float32
BF16 = jnp.bfloat16

VMEM = pl.BlockSpec(memory_space=pltpu.VMEM)
SMEM = pl.BlockSpec(memory_space=pltpu.SMEM)


def dot(a, b):
    return jnp.dot(a, b, preferred_element_type=F32)


def dot_t(a, b):
    return lax.dot_general(a, b, (((1,), (1,)), ((), ())), preferred_element_type=F32)


def normed(x):
    d = x - jnp.mean(x, axis=-1, keepdims=True)
    return d * lax.rsqrt(jnp.mean(d * d, axis=-1, keepdims=True) + epsilon)


def head_norm(u, gain):
    return u * lax.rsqrt(jnp.mean(u * u, axis=-1, keepdims=True) + epsilon) * gain


def modulate_kernel(nr, nc, image_ref, text_ref, mod_ref, out_ref):
    count, it, width = image_ref.shape
    tt = text_ref.shape[1]
    fb = width // nc

    def put(y, row, rows):
        for k in range(nc):
            part = y[:, k * fb : (k + 1) * fb]
            for r in range(nr):
                out_ref[r * nc + k, row : row + rows, :] = part

    for s in range(count):
        y = normed(image_ref[s].astype(F32))
        y = y * (1.0 + mod_ref[1, s : s + 1, :]) + mod_ref[0, s : s + 1, :]
        put(y.astype(BF16), s * it, it)
    for s in range(0, count, 2):
        both = []
        for t in (s, s + 1):
            y = normed(text_ref[t].astype(F32))
            both.append(y * (1.0 + mod_ref[4, t : t + 1, :]) + mod_ref[3, t : t + 1, :])
        put(jnp.concatenate(both, axis=0).astype(BF16), count * it + s * tt, 2 * tt)


def project_kernel(tt, image_ref, text_ref, qkv_ref, kv_ref, out_ref, text_acc):
    s = pl.program_id(0)
    heads = qkv_ref.shape[0]
    hd = out_ref.shape[-1]
    n, it, fb = image_ref.shape
    rows = n * it
    trows = n * tt

    @pl.when(s == 0)
    def _():
        text = text_ref[...].reshape(n * text_ref.shape[1], fb)
        for h in range(heads):
            text_acc[:, :, h * 2 * hd : (h + 1) * 2 * hd] = dot(text, kv_ref[h]).reshape(
                n, text_ref.shape[1], 2 * hd
            )

    image = image_ref[...].reshape(rows, fb)
    for h in range(heads):
        term = dot(image, qkv_ref[h]).astype(BF16)
        for j in range(3):
            out_ref[0, h, j * rows : (j + 1) * rows, :] = term[:, j * hd : (j + 1) * hd]
        start = pl.multiple_of(s * tt, tt)
        kv = text_acc[:, pl.ds(start, tt), h * 2 * hd : (h + 1) * 2 * hd]
        kv = kv.reshape(trows, 2 * hd).astype(BF16)
        for j in range(2):
            low = 3 * rows + j * trows
            out_ref[0, h, low : low + trows, :] = kv[:, j * hd : (j + 1) * hd]


def attend_kernel(nr, nc, rows, trows, length_ref, gain_ref, term_ref, out_ref):
    hd = term_ref.shape[-1]

    def total(low, size):
        x = term_ref[0, 0, low : low + size, :].astype(F32)
        for k in range(1, nc):
            x = x + term_ref[k, 0, low : low + size, :].astype(F32)
        return x

    queries = head_norm(total(0, rows), gain_ref[0:1, :]).astype(BF16)
    image_keys = head_norm(total(rows, rows), gain_ref[1:2, :]).astype(BF16)
    image_values = total(2 * rows, rows).astype(BF16)
    text_keys = head_norm(total(3 * rows, trows), gain_ref[2:3, :]).astype(BF16)
    text_values = total(3 * rows + trows, trows).astype(BF16)
    inv = 1.0 / math.sqrt(hd)
    live = lax.broadcasted_iota(jnp.int32, (1, trows), 1) < length_ref[0]
    expo_t = jnp.exp(dot_t(queries, text_keys) * inv) * live.astype(F32)
    expo_i = jnp.exp(dot_t(queries, image_keys) * inv)
    totals = jnp.sum(expo_t, axis=-1, keepdims=True) + jnp.sum(expo_i, axis=-1, keepdims=True)
    mixed = dot(expo_t.astype(BF16), text_values) + dot(expo_i.astype(BF16), image_values)
    heads = (mixed / totals).astype(BF16)
    size = rows // nr
    for r in range(nr):
        for c in range(nc):
            out_ref[r * nc + c, :, :] = heads[r * size : (r + 1) * size, :]


def output_kernel(nr, nc, me_ref, heads_ref, w0, w1, w2, w3, out_ref):
    me = me_ref[0]
    size = heads_ref.shape[1]
    depth = heads_ref.shape[2]
    it = size // nc
    fb = w0.shape[1]
    step = 256
    lhs = []
    for k in range(nr):
        start = lax.rem(me + nr - k, nr) * nc
        lhs.append(heads_ref[pl.ds(start, nc), :, :].reshape(nc * size, depth))
    for n in range(0, fb, step):
        total = None
        for k, w in enumerate((w0, w1, w2, w3)):
            term = dot(lhs[k], w[:, n : n + step]).astype(BF16).astype(F32)
            total = term if total is None else total + term
        attn = total.astype(BF16)
        for s in range(nc):
            for c in range(nc):
                low = s * size + c * it
                out_ref[c, s, :, n : n + step] = attn[low : low + it, :]


def final_kernel(
    image_ref, attn_ref, mod_ref, weight_ref, parts_ref, vel_ref, send_ref, final_in
):
    count, it, width = image_ref.shape
    nc = attn_ref.shape[0]
    fb = width // nc
    for s in range(count):
        pieces = []
        for k in range(nc):
            cols = slice(k * fb, (k + 1) * fb)
            x = image_ref[s, :, cols].astype(F32)
            pieces.append(x + mod_ref[2, s : s + 1, cols] * attn_ref[k, s].astype(F32))
        y = normed(jnp.concatenate(pieces, axis=-1))
        y = y * (1.0 + mod_ref[6, s : s + 1, :]) + mod_ref[5, s : s + 1, :]
        final_in[s * it : (s + 1) * it, :] = y.astype(BF16)
    velocity = dot_t(final_in[...], weight_ref[...])
    vel_ref[...] = velocity
    pairs = []
    for s in range(0, count, 2):
        low = s * it
        pairs.append(
            jnp.concatenate(
                [velocity[low : low + it, :], velocity[low + it : low + 2 * it, :]], axis=1
            )
        )
    packed = jnp.concatenate(pairs, axis=0).astype(BF16)
    half = packed.shape[0]
    for z in range(send_ref.shape[0]):
        send_ref[z, 0:half, :] = packed
        send_ref[z, half:, :] = parts_ref[...]


def guide_kernel(
    place_ref, partner_ref, guidance_ref, step_ref, same_ref, other_ref, vel_ref, latent_ref, out_ref
):
    count, it, ch = latent_ref.shape
    first = place_ref[0]
    core = place_ref[1]
    half = count // 2 * it
    for s in range(count):
        p = partner_ref[s]
        block = lax.div(p, count)
        z = lax.div(block, 2)
        slot = lax.rem(p, count)
        here = lax.rem(block, 2) == core
        row = pl.multiple_of(lax.div(slot, 2) * it, it)
        pair_same = same_ref[z, pl.ds(row, it), :].astype(F32)
        pair_other = other_ref[z, pl.ds(row, it), :].astype(F32)
        pair = jnp.where(here, pair_same, pair_other)
        mate = jnp.where(lax.rem(slot, 2) == 1, pair[:, ch:], pair[:, :ch])
        parts = jnp.where(here, same_ref[z, half:, :].astype(F32), other_ref[z, half:, :].astype(F32))
        lane = lax.broadcasted_iota(jnp.int32, parts.shape, 1)
        mate_g = jnp.where(lane == slot, parts, 0.0)
        mate_g = jnp.sum(jnp.sum(mate_g, axis=0, keepdims=True), axis=1, keepdims=True)
        own = vel_ref[s * it : (s + 1) * it, :]
        is_cond = first + s < p
        cond = jnp.where(is_cond, own, mate)
        uncond = jnp.where(is_cond, mate, own)
        g = jnp.where(is_cond, guidance_ref[s], mate_g)
        guided = uncond + g * (cond - uncond)
        ratio = jnp.sqrt(
            (jnp.mean(cond * cond, axis=-1, keepdims=True) + epsilon)
            / (jnp.mean(guided * guided, axis=-1, keepdims=True) + epsilon)
        )
        out_ref[s] = latent_ref[s] + step_ref[s] * guided * (0.7 * ratio + 0.3)


def cost(flops, size):
    return pl.CostEstimate(flops=flops, bytes_accessed=size, transcendentals=0)


def per_device(
    nb,
    nr,
    nc,
    image_tokens,
    text_tokens,
    modulation,
    qkv_weight,
    kv_weight,
    norm_gains,
    out_weight,
    final_weight,
    text_lengths,
    partner,
    guidance,
    step_size,
    latent,
):
    count, it, width = image_tokens.shape
    tt = text_tokens.shape[1]
    heads = qkv_weight.shape[1]
    hd = norm_gains.shape[1]
    ch = latent.shape[2]
    fb = width // nc
    group = nr * nc
    rows, trows = group * it, group * tt
    shape = jax.ShapeDtypeStruct
    row_index = lax.axis_index("row")
    col_index = lax.axis_index("col")
    batch_index = lax.axis_index("batch")

    mods = jnp.transpose(modulation, (1, 0, 2))
    qkv = jnp.transpose(qkv_weight, (1, 0, 2))
    kv = jnp.transpose(kv_weight, (1, 0, 2))

    sent = pl.pallas_call(
        functools.partial(modulate_kernel, nr, nc),
        out_shape=shape((group, count * (it + tt), fb), BF16),
        in_specs=[VMEM] * 3,
        out_specs=VMEM,
        cost_estimate=cost(10**7, 3 * 10**6),
        name="modulate",
    )(image_tokens, text_tokens, mods)
    tokens = lax.all_to_all(sent, ("row", "col"), split_axis=0, concat_axis=0, tiled=True)

    unit = 3 * rows + 2 * trows
    text_block = count * it // (count * tt)
    terms = pl.pallas_call(
        functools.partial(project_kernel, tt),
        grid=(count,),
        out_shape=shape((count, heads, unit, hd), BF16),
        in_specs=[
            pl.BlockSpec((group, it, fb), lambda s: (0, s, 0)),
            pl.BlockSpec((group, count * tt, fb), lambda s: (0, text_block, 0)),
            pl.BlockSpec(qkv.shape, lambda s: (0, 0, 0)),
            pl.BlockSpec(kv.shape, lambda s: (0, 0, 0)),
        ],
        out_specs=pl.BlockSpec((1, heads, unit, hd), lambda s: (s, 0, 0, 0)),
        scratch_shapes=[pltpu.VMEM((group, count * tt, heads * 2 * hd), F32)],
        cost_estimate=cost(24 * 10**8, 9 * 10**6),
        name="project",
    )(tokens, tokens, qkv, kv)

    out_local, _ = lax.optimization_barrier((out_weight.reshape(heads * hd, fb), terms))
    out_all = [out_local] + [
        lax.ppermute(out_local, "row", [(i, (i + k) % nr) for i in range(nr)]) for k in range(1, nr)
    ]
    summands = lax.all_to_all(terms, "col", split_axis=0, concat_axis=0, tiled=True)

    length = lax.dynamic_slice(text_lengths, (col_index,), (1,))
    head_out = pl.pallas_call(
        functools.partial(attend_kernel, nr, nc, rows, trows),
        grid=(heads,),
        out_shape=shape((group, rows // nr, heads * hd), BF16),
        in_specs=[
            SMEM,
            pl.BlockSpec(norm_gains.shape, lambda h: (0, 0)),
            pl.BlockSpec((nc, 1, unit, hd), lambda h: (0, h, 0, 0)),
        ],
        out_specs=pl.BlockSpec((group, rows // nr, hd), lambda h: (0, 0, h)),
        cost_estimate=cost(2 * 10**8, 4 * 10**6),
        name="attend",
    )(length, norm_gains, summands)
    head_all = lax.all_to_all(head_out, ("row", "col"), split_axis=0, concat_axis=0, tiled=True)

    attn = pl.pallas_call(
        functools.partial(output_kernel, nr, nc),
        out_shape=shape((nc, count, it, fb), BF16),
        in_specs=[SMEM] + [VMEM] * 5,
        out_specs=VMEM,
        cost_estimate=cost(6 * 10**8, 4 * 10**6),
        name="output",
    )(row_index.reshape(1), head_all, *out_all)
    attn_own = lax.all_to_all(attn, "col", split_axis=0, concat_axis=0, tiled=True)

    high = lax.reduce_precision(guidance, 8, 7)
    middle = lax.reduce_precision(guidance - high, 8, 7)
    low = guidance - high - middle
    parts = jnp.pad(jnp.stack([high, middle, low]), ((0, 5), (0, 2 * ch - count))).astype(BF16)

    zs = nb // 2
    half = count // 2 * it
    velocity, payload = pl.pallas_call(
        final_kernel,
        out_shape=(shape((count * it, ch), F32), shape((zs, half + 8, 2 * ch), BF16)),
        in_specs=[VMEM] * 5,
        out_specs=(VMEM, VMEM),
        scratch_shapes=[pltpu.VMEM((count * it, width), BF16)],
        cost_estimate=cost(3 * 10**7, 2 * 10**6),
        name="final",
    )(image_tokens, attn_own, mods, final_weight.T, parts)
    same = lax.all_to_all(
        payload,
        "batch",
        split_axis=0,
        concat_axis=0,
        tiled=True,
        axis_index_groups=[[z * 2 + core for z in range(zs)] for core in range(2)],
    )
    other = lax.ppermute(same, "batch", [(i, i ^ 1) for i in range(nb)])

    place = jnp.stack([batch_index * count, lax.rem(batch_index, 2)]).astype(jnp.int32)
    return pl.pallas_call(
        guide_kernel,
        out_shape=shape(latent.shape, F32),
        in_specs=[SMEM] * 4 + [VMEM] * 4,
        out_specs=VMEM,
        cost_estimate=cost(10**6, 10**5),
        name="guide",
    )(place, partner, guidance, step_size, same, other, velocity, latent)


def solution(mesh):
    sizes = dict(mesh.shape)
    return jax.shard_map(
        functools.partial(per_device, sizes["batch"], sizes["row"], sizes["col"]),
        mesh=mesh,
        in_specs=(
            P("batch", ("row", "col"), None),
            P("batch", ("row", "col"), None),
            P("batch", None, None),
            P("col", "row", None),
            P("col", "row", None),
            P(),
            P("row", None, "col"),
            P(),
            P("batch"),
            P("batch"),
            P("batch"),
            P("batch"),
            P("batch", ("row", "col"), None),
        ),
        out_specs=P("batch", ("row", "col"), None),
        check_vma=False,
    )
```

```python
import functools
import math

import jax
import jax.numpy as jnp
from jax import lax
from jax.experimental import pallas as pl
from jax.experimental.pallas import tpu as pltpu
from jax.sharding import PartitionSpec as P


epsilon = 1e-06
F32 = jnp.float32
BF16 = jnp.bfloat16

VMEM = pl.BlockSpec(memory_space=pltpu.VMEM)
SMEM = pl.BlockSpec(memory_space=pltpu.SMEM)


def dot(a, b):
    return jnp.dot(a, b, preferred_element_type=F32)


def dot_t(a, b):
    return lax.dot_general(a, b, (((1,), (1,)), ((), ())), preferred_element_type=F32)


def normed(x):
    d = x - jnp.mean(x, axis=-1, keepdims=True)
    return d * lax.rsqrt(jnp.mean(d * d, axis=-1, keepdims=True) + epsilon)


def head_norm(u, gain):
    return u * lax.rsqrt(jnp.mean(u * u, axis=-1, keepdims=True) + epsilon) * gain


def modulate_kernel(nr, nc, image_ref, text_ref, mod_ref, out_ref):
    count, it, width = image_ref.shape
    tt = text_ref.shape[1]
    fb = width // nc

    def put(y, row, rows):
        for k in range(nc):
            part = y[:, k * fb : (k + 1) * fb]
            for r in range(nr):
                out_ref[r * nc + k, row : row + rows, :] = part

    for s in range(count):
        y = normed(image_ref[s].astype(F32))
        y = y * (1.0 + mod_ref[1, s : s + 1, :]) + mod_ref[0, s : s + 1, :]
        put(y.astype(BF16), s * it, it)
    for s in range(0, count, 2):
        both = []
        for t in (s, s + 1):
            y = normed(text_ref[t].astype(F32))
            both.append(y * (1.0 + mod_ref[4, t : t + 1, :]) + mod_ref[3, t : t + 1, :])
        put(jnp.concatenate(both, axis=0).astype(BF16), count * it + s * tt, 2 * tt)


def project_kernel(
    tt, image_ref, text_ref, qkv_ref, kv_ref, weight_ref, out_ref, weight_out_ref, text_acc
):
    s = pl.program_id(0)
    heads = qkv_ref.shape[0]
    hd = out_ref.shape[-1]
    n, it, fb = image_ref.shape
    rows = n * it
    trows = n * tt

    @pl.when(s == 0)
    def _():
        weight_out_ref[...] = weight_ref[...]
        text = text_ref[...].reshape(n * text_ref.shape[1], fb)
        for h in range(heads):
            text_acc[:, :, h * 2 * hd : (h + 1) * 2 * hd] = dot(text, kv_ref[h]).reshape(
                n, text_ref.shape[1], 2 * hd
            )

    image = image_ref[...].reshape(rows, fb)
    for h in range(heads):
        term = dot(image, qkv_ref[h]).astype(BF16)
        for j in range(3):
            out_ref[0, h, j * rows : (j + 1) * rows, :] = term[:, j * hd : (j + 1) * hd]
        start = pl.multiple_of(s * tt, tt)
        kv = text_acc[:, pl.ds(start, tt), h * 2 * hd : (h + 1) * 2 * hd]
        kv = kv.reshape(trows, 2 * hd).astype(BF16)
        for j in range(2):
            low = 3 * rows + j * trows
            out_ref[0, h, low : low + trows, :] = kv[:, j * hd : (j + 1) * hd]


def attend_kernel(nr, nc, rows, trows, length_ref, gain_ref, term_ref, w1, w2, w3, out_ref):
    hd = term_ref.shape[-1]

    def total(low, size):
        x = term_ref[0, 0, low : low + size, :].astype(F32)
        for k in range(1, nc):
            x = x + term_ref[k, 0, low : low + size, :].astype(F32)
        return x

    queries = head_norm(total(0, rows), gain_ref[0:1, :]).astype(BF16)
    image_keys = head_norm(total(rows, rows), gain_ref[1:2, :]).astype(BF16)
    image_values = total(2 * rows, rows).astype(BF16)
    text_keys = head_norm(total(3 * rows, trows), gain_ref[2:3, :]).astype(BF16)
    text_values = total(3 * rows + trows, trows).astype(BF16)
    inv = 1.0 / math.sqrt(hd)
    live = lax.broadcasted_iota(jnp.int32, (1, trows), 1) < length_ref[0]
    expo_t = jnp.exp(dot_t(queries, text_keys) * inv) * live.astype(F32)
    expo_i = jnp.exp(dot_t(queries, image_keys) * inv)
    totals = jnp.sum(expo_t, axis=-1, keepdims=True) + jnp.sum(expo_i, axis=-1, keepdims=True)
    mixed = dot(expo_t.astype(BF16), text_values) + dot(expo_i.astype(BF16), image_values)
    heads = (mixed / totals).astype(BF16)
    size = rows // nr
    for r in range(nr):
        for c in range(nc):
            out_ref[r * nc + c, :, :] = heads[r * size : (r + 1) * size, :]


def output_kernel(nr, nc, me_ref, heads_ref, w0, w1, w2, w3, out_ref):
    me = me_ref[0]
    size = heads_ref.shape[1]
    depth = heads_ref.shape[2]
    it = size // nc
    fb = w0.shape[1]
    step = 256
    lhs = []
    for k in range(nr):
        start = lax.rem(me + nr - k, nr) * nc
        lhs.append(heads_ref[pl.ds(start, nc), :, :].reshape(nc * size, depth))
    for n in range(0, fb, step):
        total = None
        for k, w in enumerate((w0, w1, w2, w3)):
            term = dot(lhs[k], w[:, n : n + step]).astype(BF16).astype(F32)
            total = term if total is None else total + term
        attn = total.astype(BF16)
        for s in range(nc):
            for c in range(nc):
                low = s * size + c * it
                out_ref[c, s, :, n : n + step] = attn[low : low + it, :]


def final_kernel(
    image_ref, attn_ref, mod_ref, weight_ref, parts_ref, vel_ref, send_ref, final_in
):
    count, it, width = image_ref.shape
    nc = attn_ref.shape[0]
    fb = width // nc
    for s in range(count):
        pieces = []
        for k in range(nc):
            cols = slice(k * fb, (k + 1) * fb)
            x = image_ref[s, :, cols].astype(F32)
            pieces.append(x + mod_ref[2, s : s + 1, cols] * attn_ref[k, s].astype(F32))
        y = normed(jnp.concatenate(pieces, axis=-1))
        y = y * (1.0 + mod_ref[6, s : s + 1, :]) + mod_ref[5, s : s + 1, :]
        final_in[s * it : (s + 1) * it, :] = y.astype(BF16)
    velocity = dot_t(final_in[...], weight_ref[...])
    vel_ref[...] = velocity
    pairs = []
    for s in range(0, count, 2):
        low = s * it
        pairs.append(
            jnp.concatenate(
                [velocity[low : low + it, :], velocity[low + it : low + 2 * it, :]], axis=1
            )
        )
    packed = jnp.concatenate(pairs, axis=0).astype(BF16)
    half = packed.shape[0]
    for z in range(send_ref.shape[0]):
        send_ref[z, 0:half, :] = packed
        send_ref[z, half:, :] = parts_ref[...]


def guide_kernel(
    place_ref, partner_ref, guidance_ref, step_ref, same_ref, other_ref, vel_ref, latent_ref, out_ref
):
    count, it, ch = latent_ref.shape
    first = place_ref[0]
    core = place_ref[1]
    half = count // 2 * it
    for s in range(count):
        p = partner_ref[s]
        block = lax.div(p, count)
        z = lax.div(block, 2)
        slot = lax.rem(p, count)
        here = lax.rem(block, 2) == core
        row = pl.multiple_of(lax.div(slot, 2) * it, it)
        pair_same = same_ref[z, pl.ds(row, it), :].astype(F32)
        pair_other = other_ref[z, pl.ds(row, it), :].astype(F32)
        pair = jnp.where(here, pair_same, pair_other)
        mate = jnp.where(lax.rem(slot, 2) == 1, pair[:, ch:], pair[:, :ch])
        parts = jnp.where(here, same_ref[z, half:, :].astype(F32), other_ref[z, half:, :].astype(F32))
        lane = lax.broadcasted_iota(jnp.int32, parts.shape, 1)
        mate_g = jnp.where(lane == slot, parts, 0.0)
        mate_g = jnp.sum(jnp.sum(mate_g, axis=0, keepdims=True), axis=1, keepdims=True)
        own = vel_ref[s * it : (s + 1) * it, :]
        is_cond = first + s < p
        cond = jnp.where(is_cond, own, mate)
        uncond = jnp.where(is_cond, mate, own)
        g = jnp.where(is_cond, guidance_ref[s], mate_g)
        guided = uncond + g * (cond - uncond)
        ratio = jnp.sqrt(
            (jnp.mean(cond * cond, axis=-1, keepdims=True) + epsilon)
            / (jnp.mean(guided * guided, axis=-1, keepdims=True) + epsilon)
        )
        out_ref[s] = latent_ref[s] + step_ref[s] * guided * (0.7 * ratio + 0.3)


def params(mib):
    return pltpu.CompilerParams(vmem_limit_bytes=mib * 2**20)


def cost(flops, size):
    return pl.CostEstimate(flops=flops, bytes_accessed=size, transcendentals=0)


def per_device(
    nb,
    nr,
    nc,
    image_tokens,
    text_tokens,
    modulation,
    qkv_weight,
    kv_weight,
    norm_gains,
    out_weight,
    final_weight,
    text_lengths,
    partner,
    guidance,
    step_size,
    latent,
):
    count, it, width = image_tokens.shape
    tt = text_tokens.shape[1]
    heads = qkv_weight.shape[1]
    hd = norm_gains.shape[1]
    ch = latent.shape[2]
    fb = width // nc
    group = nr * nc
    rows, trows = group * it, group * tt
    shape = jax.ShapeDtypeStruct
    row_index = lax.axis_index("row")
    col_index = lax.axis_index("col")
    batch_index = lax.axis_index("batch")

    mods = jnp.transpose(modulation, (1, 0, 2))
    qkv = jnp.transpose(qkv_weight, (1, 0, 2))
    kv = jnp.transpose(kv_weight, (1, 0, 2))

    sent = pl.pallas_call(
        functools.partial(modulate_kernel, nr, nc),
        out_shape=shape((group, count * (it + tt), fb), BF16),
        in_specs=[VMEM] * 3,
        out_specs=VMEM,
        cost_estimate=cost(10**7, 3 * 10**6),
        compiler_params=params(10),
        name="modulate",
    )(image_tokens, text_tokens, mods)
    tokens = lax.all_to_all(sent, ("row", "col"), split_axis=0, concat_axis=0, tiled=True)

    unit = 3 * rows + 2 * trows
    text_block = count * it // (count * tt)
    out_local = out_weight.reshape(heads * hd, fb)
    terms, out_sent = pl.pallas_call(
        functools.partial(project_kernel, tt),
        grid=(count,),
        out_shape=(shape((count, heads, unit, hd), BF16), shape(out_local.shape, BF16)),
        in_specs=[
            pl.BlockSpec((group, it, fb), lambda s: (0, s, 0)),
            pl.BlockSpec((group, count * tt, fb), lambda s: (0, text_block, 0)),
            pl.BlockSpec(qkv.shape, lambda s: (0, 0, 0)),
            pl.BlockSpec(kv.shape, lambda s: (0, 0, 0)),
            pl.BlockSpec(out_local.shape, lambda s: (0, 0)),
        ],
        out_specs=(
            pl.BlockSpec((1, heads, unit, hd), lambda s: (s, 0, 0, 0)),
            pl.BlockSpec(out_local.shape, lambda s: (0, 0)),
        ),
        scratch_shapes=[pltpu.VMEM((group, count * tt, heads * 2 * hd), F32)],
        cost_estimate=cost(24 * 10**8, 9 * 10**6),
        compiler_params=params(16),
        name="project",
    )(tokens, tokens, qkv, kv, out_local)

    out_all = [out_local] + [
        lax.ppermute(out_sent, "row", [(i, (i + k) % nr) for i in range(nr)]) for k in range(1, nr)
    ]
    summands = lax.all_to_all(terms, "col", split_axis=0, concat_axis=0, tiled=True)

    length = lax.dynamic_slice(text_lengths, (col_index,), (1,))
    head_out = pl.pallas_call(
        functools.partial(attend_kernel, nr, nc, rows, trows),
        grid=(heads,),
        out_shape=shape((group, rows // nr, heads * hd), BF16),
        in_specs=[
            SMEM,
            pl.BlockSpec(norm_gains.shape, lambda h: (0, 0)),
            pl.BlockSpec((nc, 1, unit, hd), lambda h: (0, h, 0, 0)),
        ]
        + [pl.BlockSpec(memory_space=pl.ANY)] * (nr - 1),
        out_specs=pl.BlockSpec((group, rows // nr, hd), lambda h: (0, 0, h)),
        cost_estimate=cost(2 * 10**8, 4 * 10**6),
        compiler_params=params(12),
        name="attend",
    )(length, norm_gains, summands, *out_all[1:])
    head_all = lax.all_to_all(head_out, ("row", "col"), split_axis=0, concat_axis=0, tiled=True)

    attn = pl.pallas_call(
        functools.partial(output_kernel, nr, nc),
        out_shape=shape((nc, count, it, fb), BF16),
        in_specs=[SMEM] + [VMEM] * 5,
        out_specs=VMEM,
        cost_estimate=cost(6 * 10**8, 4 * 10**6),
        compiler_params=params(10),
        name="output",
    )(row_index.reshape(1), head_all, *out_all)
    attn_own = lax.all_to_all(attn, "col", split_axis=0, concat_axis=0, tiled=True)

    high = lax.reduce_precision(guidance, 8, 7)
    middle = lax.reduce_precision(guidance - high, 8, 7)
    low = guidance - high - middle
    parts = jnp.pad(jnp.stack([high, middle, low]), ((0, 5), (0, 2 * ch - count))).astype(BF16)

    zs = nb // 2
    half = count // 2 * it
    velocity, payload = pl.pallas_call(
        final_kernel,
        out_shape=(shape((count * it, ch), F32), shape((zs, half + 8, 2 * ch), BF16)),
        in_specs=[VMEM] * 5,
        out_specs=(VMEM, VMEM),
        scratch_shapes=[pltpu.VMEM((count * it, width), BF16)],
        cost_estimate=cost(3 * 10**7, 2 * 10**6),
        compiler_params=params(10),
        name="final",
    )(image_tokens, attn_own, mods, final_weight.T, parts)
    same = lax.all_to_all(
        payload,
        "batch",
        split_axis=0,
        concat_axis=0,
        tiled=True,
        axis_index_groups=[[z * 2 + core for z in range(zs)] for core in range(2)],
    )
    other = lax.ppermute(same, "batch", [(i, i ^ 1) for i in range(nb)])

    place = jnp.stack([batch_index * count, lax.rem(batch_index, 2)]).astype(jnp.int32)
    return pl.pallas_call(
        guide_kernel,
        out_shape=shape(latent.shape, F32),
        in_specs=[SMEM] * 4 + [VMEM] * 4,
        out_specs=VMEM,
        cost_estimate=cost(10**6, 10**5),
        compiler_params=params(6),
        name="guide",
    )(place, partner, guidance, step_size, same, other, velocity, latent)


def solution(mesh):
    sizes = dict(mesh.shape)
    return jax.shard_map(
        functools.partial(per_device, sizes["batch"], sizes["row"], sizes["col"]),
        mesh=mesh,
        in_specs=(
            P("batch", ("row", "col"), None),
            P("batch", ("row", "col"), None),
            P("batch", None, None),
            P("col", "row", None),
            P("col", "row", None),
            P(),
            P("row", None, "col"),
            P(),
            P("batch"),
            P("batch"),
            P("batch"),
            P("batch"),
            P("batch", ("row", "col"), None),
        ),
        out_specs=P("batch", ("row", "col"), None),
        check_vma=False,
    )
```

```python
import functools
import math

import jax
import jax.numpy as jnp
from jax import lax
from jax.experimental import pallas as pl
from jax.experimental.pallas import tpu as pltpu
from jax.sharding import PartitionSpec as P


epsilon = 1e-06
F32 = jnp.float32
BF16 = jnp.bfloat16

VMEM = pl.BlockSpec(memory_space=pltpu.VMEM)
SMEM = pl.BlockSpec(memory_space=pltpu.SMEM)
HBM = pl.BlockSpec(memory_space=pltpu.HBM)


def dot(a, b):
    return jnp.dot(a, b, preferred_element_type=F32)


def dot_t(a, b):
    return lax.dot_general(a, b, (((1,), (1,)), ((), ())), preferred_element_type=F32)


def normed(x):
    d = x - jnp.mean(x, axis=-1, keepdims=True)
    return d * lax.rsqrt(jnp.mean(d * d, axis=-1, keepdims=True) + epsilon)


def head_norm(u, gain):
    return u * lax.rsqrt(jnp.mean(u * u, axis=-1, keepdims=True) + epsilon) * gain


def modulate_kernel(
    nr, nc, image_hbm, text_hbm, mod_hbm, out_ref, image_ref, text_ref, mod_ref, sem
):
    copies = [
        pltpu.make_async_copy(src, dst, sem.at[k])
        for k, (src, dst) in enumerate(
            ((image_hbm, image_ref), (mod_hbm, mod_ref), (text_hbm, text_ref))
        )
    ]
    for copy in copies:
        copy.start()
    count, it, width = image_ref.shape
    tt = text_ref.shape[1]
    fb = width // nc

    def put(y, row, rows):
        for k in range(nc):
            part = y[:, k * fb : (k + 1) * fb]
            for r in range(nr):
                out_ref[r * nc + k, row : row + rows, :] = part

    copies[0].wait()
    copies[1].wait()
    for s in range(count):
        y = normed(image_ref[s].astype(F32))
        y = y * (1.0 + mod_ref[1, s : s + 1, :]) + mod_ref[0, s : s + 1, :]
        put(y.astype(BF16), s * it, it)
    copies[2].wait()
    for s in range(0, count, 2):
        both = []
        for t in (s, s + 1):
            y = normed(text_ref[t].astype(F32))
            both.append(y * (1.0 + mod_ref[4, t : t + 1, :]) + mod_ref[3, t : t + 1, :])
        put(jnp.concatenate(both, axis=0).astype(BF16), count * it + s * tt, 2 * tt)


def project_kernel(
    tt, image_ref, text_ref, qkv_ref, kv_ref, weight_ref, out_ref, weight_out_ref, text_acc
):
    s = pl.program_id(0)
    heads = qkv_ref.shape[0]
    hd = out_ref.shape[-1]
    n, it, fb = image_ref.shape
    rows = n * it
    trows = n * tt

    @pl.when(s == 0)
    def _():
        weight_out_ref[...] = weight_ref[...]
        text = text_ref[...].reshape(n * text_ref.shape[1], fb)
        for h in range(heads):
            text_acc[:, :, h * 2 * hd : (h + 1) * 2 * hd] = dot(text, kv_ref[h]).reshape(
                n, text_ref.shape[1], 2 * hd
            )

    image = image_ref[...].reshape(rows, fb)
    for h in range(heads):
        term = dot(image, qkv_ref[h]).astype(BF16)
        for j in range(3):
            out_ref[0, h, j * rows : (j + 1) * rows, :] = term[:, j * hd : (j + 1) * hd]
        start = pl.multiple_of(s * tt, tt)
        kv = text_acc[:, pl.ds(start, tt), h * 2 * hd : (h + 1) * 2 * hd]
        kv = kv.reshape(trows, 2 * hd).astype(BF16)
        for j in range(2):
            low = 3 * rows + j * trows
            out_ref[0, h, low : low + trows, :] = kv[:, j * hd : (j + 1) * hd]


def attend_kernel(nr, nc, rows, trows, length_ref, gain_ref, term_ref, w1, w2, w3, out_ref):
    hd = term_ref.shape[-1]

    def total(low, size):
        x = term_ref[0, 0, low : low + size, :].astype(F32)
        for k in range(1, nc):
            x = x + term_ref[k, 0, low : low + size, :].astype(F32)
        return x

    queries = head_norm(total(0, rows), gain_ref[0:1, :]).astype(BF16)
    image_keys = head_norm(total(rows, rows), gain_ref[1:2, :]).astype(BF16)
    image_values = total(2 * rows, rows).astype(BF16)
    text_keys = head_norm(total(3 * rows, trows), gain_ref[2:3, :]).astype(BF16)
    text_values = total(3 * rows + trows, trows).astype(BF16)
    inv = 1.0 / math.sqrt(hd)
    live = lax.broadcasted_iota(jnp.int32, (1, trows), 1) < length_ref[0]
    expo_t = jnp.exp(dot_t(queries, text_keys) * inv) * live.astype(F32)
    expo_i = jnp.exp(dot_t(queries, image_keys) * inv)
    totals = jnp.sum(expo_t, axis=-1, keepdims=True) + jnp.sum(expo_i, axis=-1, keepdims=True)
    mixed = dot(expo_t.astype(BF16), text_values) + dot(expo_i.astype(BF16), image_values)
    heads = (mixed / totals).astype(BF16)
    size = rows // nr
    for r in range(nr):
        for c in range(nc):
            out_ref[r * nc + c, :, :] = heads[r * size : (r + 1) * size, :]


def output_kernel(nr, nc, me_ref, heads_ref, w0, w1, w2, w3, out_ref):
    me = me_ref[0]
    size = heads_ref.shape[1]
    depth = heads_ref.shape[2]
    it = size // nc
    fb = w0.shape[1]
    step = 256
    lhs = []
    for k in range(nr):
        start = lax.rem(me + nr - k, nr) * nc
        lhs.append(heads_ref[pl.ds(start, nc), :, :].reshape(nc * size, depth))
    for n in range(0, fb, step):
        total = None
        for k, w in enumerate((w0, w1, w2, w3)):
            term = dot(lhs[k], w[:, n : n + step]).astype(BF16).astype(F32)
            total = term if total is None else total + term
        attn = total.astype(BF16)
        for s in range(nc):
            for c in range(nc):
                low = s * size + c * it
                out_ref[c, s, :, n : n + step] = attn[low : low + it, :]


def final_kernel(
    image_ref, attn_ref, mod_ref, weight_ref, parts_ref, vel_ref, send_ref, final_in
):
    count, it, width = image_ref.shape
    nc = attn_ref.shape[0]
    fb = width // nc
    for s in range(count):
        pieces = []
        for k in range(nc):
            cols = slice(k * fb, (k + 1) * fb)
            x = image_ref[s, :, cols].astype(F32)
            pieces.append(x + mod_ref[2, s : s + 1, cols] * attn_ref[k, s].astype(F32))
        y = normed(jnp.concatenate(pieces, axis=-1))
        y = y * (1.0 + mod_ref[6, s : s + 1, :]) + mod_ref[5, s : s + 1, :]
        final_in[s * it : (s + 1) * it, :] = y.astype(BF16)
    velocity = dot_t(final_in[...], weight_ref[...])
    vel_ref[...] = velocity
    pairs = []
    for s in range(0, count, 2):
        low = s * it
        pairs.append(
            jnp.concatenate(
                [velocity[low : low + it, :], velocity[low + it : low + 2 * it, :]], axis=1
            )
        )
    packed = jnp.concatenate(pairs, axis=0).astype(BF16)
    half = packed.shape[0]
    for z in range(send_ref.shape[0]):
        send_ref[z, 0:half, :] = packed
        send_ref[z, half:, :] = parts_ref[...]


def guide_kernel(
    place_ref, partner_ref, guidance_ref, step_ref, same_ref, other_ref, vel_ref, latent_ref, out_ref
):
    count, it, ch = latent_ref.shape
    first = place_ref[0]
    core = place_ref[1]
    half = count // 2 * it
    for s in range(count):
        p = partner_ref[s]
        block = lax.div(p, count)
        z = lax.div(block, 2)
        slot = lax.rem(p, count)
        here = lax.rem(block, 2) == core
        row = pl.multiple_of(lax.div(slot, 2) * it, it)
        pair_same = same_ref[z, pl.ds(row, it), :].astype(F32)
        pair_other = other_ref[z, pl.ds(row, it), :].astype(F32)
        pair = jnp.where(here, pair_same, pair_other)
        mate = jnp.where(lax.rem(slot, 2) == 1, pair[:, ch:], pair[:, :ch])
        parts = jnp.where(here, same_ref[z, half:, :].astype(F32), other_ref[z, half:, :].astype(F32))
        lane = lax.broadcasted_iota(jnp.int32, parts.shape, 1)
        mate_g = jnp.where(lane == slot, parts, 0.0)
        mate_g = jnp.sum(jnp.sum(mate_g, axis=0, keepdims=True), axis=1, keepdims=True)
        own = vel_ref[s * it : (s + 1) * it, :]
        is_cond = first + s < p
        cond = jnp.where(is_cond, own, mate)
        uncond = jnp.where(is_cond, mate, own)
        g = jnp.where(is_cond, guidance_ref[s], mate_g)
        guided = uncond + g * (cond - uncond)
        ratio = jnp.sqrt(
            (jnp.mean(cond * cond, axis=-1, keepdims=True) + epsilon)
            / (jnp.mean(guided * guided, axis=-1, keepdims=True) + epsilon)
        )
        out_ref[s] = latent_ref[s] + step_ref[s] * guided * (0.7 * ratio + 0.3)


def params(mib):
    return pltpu.CompilerParams(vmem_limit_bytes=mib * 2**20)


def cost(flops, size):
    return pl.CostEstimate(flops=flops, bytes_accessed=size, transcendentals=0)


def per_device(
    nb,
    nr,
    nc,
    image_tokens,
    text_tokens,
    modulation,
    qkv_weight,
    kv_weight,
    norm_gains,
    out_weight,
    final_weight,
    text_lengths,
    partner,
    guidance,
    step_size,
    latent,
):
    count, it, width = image_tokens.shape
    tt = text_tokens.shape[1]
    heads = qkv_weight.shape[1]
    hd = norm_gains.shape[1]
    ch = latent.shape[2]
    fb = width // nc
    group = nr * nc
    rows, trows = group * it, group * tt
    shape = jax.ShapeDtypeStruct
    row_index = lax.axis_index("row")
    col_index = lax.axis_index("col")
    batch_index = lax.axis_index("batch")

    mods = jnp.transpose(modulation, (1, 0, 2))
    qkv = jnp.transpose(qkv_weight, (1, 0, 2))
    kv = jnp.transpose(kv_weight, (1, 0, 2))

    sent = pl.pallas_call(
        functools.partial(modulate_kernel, nr, nc),
        out_shape=shape((group, count * (it + tt), fb), BF16),
        in_specs=[HBM] * 3,
        out_specs=VMEM,
        scratch_shapes=[
            pltpu.VMEM(image_tokens.shape, BF16),
            pltpu.VMEM(text_tokens.shape, BF16),
            pltpu.VMEM(mods.shape, F32),
            pltpu.SemaphoreType.DMA((3,)),
        ],
        cost_estimate=cost(10**7, 3 * 10**6),
        compiler_params=params(60),
        name="modulate",
    )(image_tokens, text_tokens, mods)
    tokens = lax.all_to_all(sent, ("row", "col"), split_axis=0, concat_axis=0, tiled=True)

    unit = 3 * rows + 2 * trows
    text_block = count * it // (count * tt)
    out_local = out_weight.reshape(heads * hd, fb)
    terms, out_sent = pl.pallas_call(
        functools.partial(project_kernel, tt),
        grid=(count,),
        out_shape=(pltpu.HBM((count, heads, unit, hd), BF16), pltpu.HBM(out_local.shape, BF16)),
        in_specs=[
            pl.BlockSpec((group, it, fb), lambda s: (0, s, 0)),
            pl.BlockSpec((group, count * tt, fb), lambda s: (0, text_block, 0)),
            pl.BlockSpec(qkv.shape, lambda s: (0, 0, 0)),
            pl.BlockSpec(kv.shape, lambda s: (0, 0, 0)),
            pl.BlockSpec(out_local.shape, lambda s: (0, 0)),
        ],
        out_specs=(
            pl.BlockSpec((1, heads, unit, hd), lambda s: (s, 0, 0, 0)),
            pl.BlockSpec(out_local.shape, lambda s: (0, 0)),
        ),
        scratch_shapes=[pltpu.VMEM((group, count * tt, heads * 2 * hd), F32)],
        cost_estimate=cost(24 * 10**8, 9 * 10**6),
        compiler_params=params(16),
        name="project",
    )(tokens, tokens, qkv, kv, out_local)

    out_all = [out_sent] + [
        lax.ppermute(out_sent, "row", [(i, (i + k) % nr) for i in range(nr)]) for k in range(1, nr)
    ]
    summands = lax.all_to_all(terms, "col", split_axis=0, concat_axis=0, tiled=True)

    length = lax.dynamic_slice(text_lengths, (col_index,), (1,))
    head_out = pl.pallas_call(
        functools.partial(attend_kernel, nr, nc, rows, trows),
        grid=(heads,),
        out_shape=pltpu.HBM((group, rows // nr, heads * hd), BF16),
        in_specs=[
            SMEM,
            pl.BlockSpec(norm_gains.shape, lambda h: (0, 0)),
            pl.BlockSpec((nc, 1, unit, hd), lambda h: (0, h, 0, 0)),
        ]
        + [pl.BlockSpec(memory_space=pl.ANY)] * (nr - 1),
        out_specs=pl.BlockSpec((group, rows // nr, hd), lambda h: (0, 0, h)),
        cost_estimate=cost(2 * 10**8, 4 * 10**6),
        compiler_params=params(12),
        name="attend",
    )(length, norm_gains, summands, *out_all[1:])
    head_all = lax.all_to_all(head_out, ("row", "col"), split_axis=0, concat_axis=0, tiled=True)

    attn = pl.pallas_call(
        functools.partial(output_kernel, nr, nc),
        out_shape=shape((nc, count, it, fb), BF16),
        in_specs=[SMEM] + [VMEM] * 5,
        out_specs=VMEM,
        cost_estimate=cost(6 * 10**8, 4 * 10**6),
        compiler_params=params(10),
        name="output",
    )(row_index.reshape(1), head_all, *out_all)
    attn_own = lax.all_to_all(attn, "col", split_axis=0, concat_axis=0, tiled=True)

    high = lax.reduce_precision(guidance, 8, 7)
    middle = lax.reduce_precision(guidance - high, 8, 7)
    low = guidance - high - middle
    parts = jnp.pad(jnp.stack([high, middle, low]), ((0, 5), (0, 2 * ch - count))).astype(BF16)

    zs = nb // 2
    half = count // 2 * it
    velocity, payload = pl.pallas_call(
        final_kernel,
        out_shape=(shape((count * it, ch), F32), shape((zs, half + 8, 2 * ch), BF16)),
        in_specs=[VMEM] * 5,
        out_specs=(VMEM, VMEM),
        scratch_shapes=[pltpu.VMEM((count * it, width), BF16)],
        cost_estimate=cost(3 * 10**7, 2 * 10**6),
        compiler_params=params(10),
        name="final",
    )(image_tokens, attn_own, mods, final_weight.T, parts)
    same = lax.all_to_all(
        payload,
        "batch",
        split_axis=0,
        concat_axis=0,
        tiled=True,
        axis_index_groups=[[z * 2 + core for z in range(zs)] for core in range(2)],
    )
    other = lax.ppermute(same, "batch", [(i, i ^ 1) for i in range(nb)])

    place = jnp.stack([batch_index * count, lax.rem(batch_index, 2)]).astype(jnp.int32)
    return pl.pallas_call(
        guide_kernel,
        out_shape=shape(latent.shape, F32),
        in_specs=[SMEM] * 4 + [VMEM] * 4,
        out_specs=VMEM,
        cost_estimate=cost(10**6, 10**5),
        compiler_params=params(6),
        name="guide",
    )(place, partner, guidance, step_size, same, other, velocity, latent)


def solution(mesh):
    sizes = dict(mesh.shape)
    return jax.shard_map(
        functools.partial(per_device, sizes["batch"], sizes["row"], sizes["col"]),
        mesh=mesh,
        in_specs=(
            P("batch", ("row", "col"), None),
            P("batch", ("row", "col"), None),
            P("batch", None, None),
            P("col", "row", None),
            P("col", "row", None),
            P(),
            P("row", None, "col"),
            P(),
            P("batch"),
            P("batch"),
            P("batch"),
            P("batch"),
            P("batch", ("row", "col"), None),
        ),
        out_specs=P("batch", ("row", "col"), None),
        check_vma=False,
    )
```
